32 devices in a mesh: ctx: 8 (over y, x, core), head: 4 (over z).
Axes of the slice: x: 2, y: 2, z: 4, core: 2. Of those that a mesh axis runs over, the one named last changes fastest.
Arguments:
- main_query: bfloat16 [1024, 73728], P('ctx', 'head'), as said below
- latents: bfloat16 [512, 576], P('ctx'), may hold values from -6 to 6, as said below
- idx_query: bfloat16 [1024, 8192], P('ctx'), as said below
- idx_weight: float32 [1024, 64], P('ctx'), may hold values from -9 to 9
- idx_keys: bfloat16 [512, 128], P('ctx'), may hold values from -6 to 6, as said below
- kl_cotangent: float32 [1024], P('ctx'), may hold values from 4 to 64
- query_start: int32 [1], replicated, may hold values from 256 to 511
- key_start: int32 [1], replicated, may hold values from 0 to 255
Outputs:
- grad_query: float32 [1024, 8192], P('ctx', 'head')
- grad_weight: float32 [1024, 64], P('ctx', 'head')
- grad_keys: float32 [512, 128], P(('ctx', 'head'))
The draws below stay inside these ranges and needn't reach their ends.
Inputs may be any that keep to these rules, and one draw needn't show every extreme that they name: `latents`: saved latent keys of order one. `idx_keys`: indexer keys of order one. `main_query`: attention queries; a few rows may be large. `idx_query`: indexer queries; a few rows may be large.
All inputs are finite; a program needn't handle non-finite values.
Results may differ from the reference program's by a relative error of at most 0.02.
Values may be sent and summed in bfloat16 or wider, within the bound.
A program may use at most 128 MiB of HBM per device.

```python
import math
import jax
import jax.numpy as jnp
from jax import lax

LATENT = 576
MAIN_HEADS = 128
IDX_HEADS = 64
IDX_DIM = 128
QUERY_DEV = 128
QUERIES = 1024
KEYS = 512
N_CTX = 8


def slab_draw(key):
    key_latent = jax.random.fold_in(key, 71)
    key_index = jax.random.fold_in(key, 72)
    key_main = jax.random.fold_in(key, 73)
    key_query = jax.random.fold_in(key, 74)
    key_weight = jax.random.fold_in(key, 75)
    latent_table = jnp.clip(jax.random.normal(key_latent, (KEYS, LATENT), jnp.float32), -6.0, 6.0)
    index_table = jnp.clip(jax.random.normal(key_index, (KEYS, IDX_DIM), jnp.float32), -6.0, 6.0)
    main_table = jnp.clip(jax.random.normal(key_main, (QUERIES, MAIN_HEADS, LATENT), jnp.float32), -6.0, 6.0)
    query_table = jnp.clip(jax.random.normal(key_query, (QUERIES, IDX_HEADS, IDX_DIM), jnp.float32), -6.0, 6.0)
    weight_table = 0.5 * jnp.clip(jax.random.normal(key_weight, (QUERIES, IDX_HEADS), jnp.float32), -6.0, 6.0)
    return (latent_table, index_table, main_table.reshape(QUERIES, MAIN_HEADS * LATENT), query_table.reshape(QUERIES, IDX_HEADS * IDX_DIM), weight_table)


def draw_latents(key, part):
    return slab_draw(key)[0].astype(jnp.bfloat16)


def draw_idx_keys(key, part):
    return slab_draw(key)[1].astype(jnp.bfloat16)


def draw_main_query(key, part):
    return slab_draw(key)[2].astype(jnp.bfloat16)


def draw_idx_query(key, part):
    return slab_draw(key)[3].astype(jnp.bfloat16)


def draw_idx_weight(key, part):
    return slab_draw(key)[4]


def shard_levels(rng, shape, shards, smallest, top_value):
    loudness, own = 1.0, jax.random.fold_in(rng, 6)
    for position, shards_of in shards:
        heights = jnp.exp(jax.random.uniform(jax.random.fold_in(own, position), (shards_of,), jnp.float32, smallest / len(shards), top_value / len(shards)))
        loudness = loudness * jnp.repeat(heights, shape[position] // shards_of).reshape([-1 if axis == position else 1 for axis in range(len(shape))])
    return loudness


def setup_inputs(seed: int = 0) -> dict:
    streams_of = jax.random.split(jax.random.key(seed), 9)
    main_query = draw_main_query(jax.random.fold_in(streams_of[8], 71), 0)
    latents = draw_latents(jax.random.fold_in(streams_of[8], 71), 0)
    idx_query = draw_idx_query(jax.random.fold_in(streams_of[8], 71), 0)
    idx_weight = draw_idx_weight(jax.random.fold_in(streams_of[8], 71), 0)
    idx_keys = draw_idx_keys(jax.random.fold_in(streams_of[8], 71), 0)
    kl_cotangent = jnp.clip(jnp.exp(math.log(64.0) - 2.7725887 * jax.random.uniform(streams_of[5], (QUERIES,), jnp.float32) ** shard_levels(streams_of[5], (QUERIES,), ((0, 8),), -0.2, 0.2)), 4.0, 64.0)
    query_start = jax.random.randint(streams_of[6], (1,), KEYS // 2, KEYS).astype(jnp.int32)
    key_start = jax.random.randint(streams_of[7], (1,), 0, KEYS // 2).astype(jnp.int32)
    return dict(main_query=main_query, latents=latents, idx_query=idx_query, idx_weight=idx_weight, idx_keys=idx_keys, kl_cotangent=kl_cotangent, query_start=query_start, key_start=key_start)


NEGATIVE = -1e30
MAIN_SCALE = 192.0 ** -0.5


def masked_softmax(values, visible):
    values = jnp.where(visible, values, NEGATIVE)
    largest = jnp.max(values, axis=-1, keepdims=True)
    weights = jnp.where(visible, jnp.exp(values - largest), 0.0)
    return weights / jnp.sum(weights, axis=-1, keepdims=True)


def reference(main_query, latents, idx_query, idx_weight, idx_keys, kl_cotangent, query_start, key_start):
    queries_main = main_query.reshape(QUERIES, MAIN_HEADS, LATENT)
    queries_index = idx_query.reshape(QUERIES, IDX_HEADS, IDX_DIM)
    query_position = query_start[0] + jnp.arange(QUERIES, dtype=jnp.int32)
    key_position = key_start[0] + jnp.arange(KEYS, dtype=jnp.int32)
    scale = IDX_DIM ** -0.5

    def one_block(key_total, block_index):
        start = (block_index * QUERY_DEV).astype(jnp.int32)
        block_main = lax.dynamic_slice_in_dim(queries_main, start, QUERY_DEV, 0)
        block_index_q = lax.dynamic_slice_in_dim(queries_index, start, QUERY_DEV, 0)
        block_weight = lax.dynamic_slice_in_dim(idx_weight, start, QUERY_DEV, 0)
        block_cotangent = lax.dynamic_slice_in_dim(kl_cotangent, start, QUERY_DEV, 0)
        block_position = lax.dynamic_slice_in_dim(query_position, start, QUERY_DEV, 0)
        visible = key_position[None, :] <= block_position[:, None]

        def add_head(head_number, totals):
            head_query = lax.dynamic_index_in_dim(block_main, head_number, 1, keepdims=False)
            scores = jnp.dot(head_query, latents.T, preferred_element_type=jnp.float32) * MAIN_SCALE
            return totals + masked_softmax(scores, visible)

        totals = lax.fori_loop(0, MAIN_HEADS, add_head, jnp.zeros((QUERY_DEV, KEYS), jnp.float32))
        target = totals / MAIN_HEADS
        inner = jnp.einsum("bjd,kd->bjk", block_index_q.astype(jnp.float32), idx_keys.astype(jnp.float32)) * scale
        active = jnp.maximum(inner, 0.0)
        logits = jnp.sum(block_weight[:, :, None] * active, axis=1)
        chance = masked_softmax(logits, visible)
        upstream = block_cotangent[:, None] * (chance - target)
        grad_inner = jnp.where(inner > 0.0, upstream[:, None, :] * block_weight[:, :, None], 0.0).astype(jnp.bfloat16)
        weight_grad = jnp.sum(upstream[:, None, :] * active, axis=-1)
        query_grad = jnp.einsum("bjk,kd->bjd", grad_inner.astype(jnp.float32), idx_keys.astype(jnp.float32)) * scale
        key_grad = jnp.einsum("bjk,bjd->kd", grad_inner.astype(jnp.float32), block_index_q.astype(jnp.float32)) * scale
        return key_total + key_grad, (query_grad.reshape(QUERY_DEV, IDX_HEADS * IDX_DIM), weight_grad)

    key_total, (query_grads, weight_grads) = lax.scan(one_block, jnp.zeros((KEYS, IDX_DIM), jnp.float32), jnp.arange(N_CTX, dtype=jnp.int32))
    grad_query = query_grads.reshape(QUERIES, IDX_HEADS * IDX_DIM)
    grad_weight = weight_grads.reshape(QUERIES, IDX_HEADS)
    return grad_query, grad_weight, key_total
```

```python
import functools
import math

import jax
import jax.numpy as jnp
from jax import lax
from jax.experimental import pallas as pl
from jax.experimental.pallas import tpu as pltpu
from jax.sharding import PartitionSpec as P

NEGATIVE = -1e30
LOG2E = math.log2(math.e)
MAIN_SCALE = 192.0 ** (-0.5)
MESH = pl.DeviceIdType.MESH
NT = (((1,), (1,)), ((), ()))


def kernel(
    n, hc, qs_ref, ks_ref, main_ref, lat_ref, iq_ref, w_ref, ik_ref, cot_ref,
    gq_ref, gw_ref, gk_ref,
    q_buf, iql, iqg, lat_all, ik_all, k_even, k_odd, t_send, t_recv, u_send, u_all, w_all, gains_all, gw_wide, dk, dk_send, dk_recv, z_send, z_recv,
    q_sem, i_sem, lat_s, lat_r, lat_f, ik_s, ik_r, ik_f, t_s, t_r, u_s, u_r, d_s, d_r, z_s, z_r,
):
    me = lax.axis_index("ctx")
    h = lax.axis_index("head")
    pairs, rows, pair_width = q_buf.shape
    width = pair_width // 2
    block, key_width = lat_ref.shape[0], k_even.shape[1]
    keys = n * block
    heads = w_ref.shape[0]
    dim = ik_ref.shape[1]
    part = rows // hc
    own_heads = heads // hc
    scale = dim ** (-0.5)
    shift = pair_width - key_width

    loads = [
        pltpu.make_async_copy(iq_ref.at[pl.ds(pl.multiple_of(h * part, part), part), :], iql, i_sem.at[0]),
        pltpu.make_async_copy(
            iq_ref.at[:, pl.ds(pl.multiple_of(h * own_heads * dim, own_heads * dim), own_heads * dim)], iqg, i_sem.at[1]
        ),
    ]
    q_loads = [
        pltpu.make_async_copy(main_ref.at[:, pl.ds(p * pair_width, pair_width)], q_buf.at[p], q_sem.at[p])
        for p in range(pairs)
    ]
    for copy in loads + q_loads:
        copy.start()

    barrier = pltpu.get_barrier_semaphore()
    for t in range(1, n):
        pl.semaphore_signal(barrier, inc=1, device_id={"ctx": lax.rem(me + t, n)}, device_id_type=MESH)
    for k in range(1, hc):
        pl.semaphore_signal(barrier, inc=1, device_id={"head": lax.rem(h + k, hc)}, device_id_type=MESH)
    pl.semaphore_wait(barrier, n - 1 + hc - 1)

    parity = lax.rem(me, 2)
    partner = me + 1 - 2 * parity
    if hc == 4:
        others = [hc - 1 - h, lax.rem(h + 2, hc), h + 1 - 2 * lax.rem(h, 2)]
        sources = others
    else:
        others = [lax.rem(h + k, hc) for k in range(1, hc)]
        sources = [lax.rem(h - k + hc, hc) for k in range(1, hc)]

    def push(src, dst, at, to, send, recv):
        return pltpu.make_async_remote_copy(
            src_ref=src, dst_ref=dst.at[at], send_sem=send, recv_sem=recv.at[at],
            device_id={"ctx": to}, device_id_type=MESH,
        )

    def spread(src, dst, send, recv, forward):
        direct, relays, arrivals = [], [], []
        own = push(src, dst, me, partner, forward.at[0], recv)
        if n == 8:
            beside = me + 2 - 4 * lax.rem(me // 2, 2)
            across = me + 4 - 8 * (me // 4)
            far = beside + across - me
            source = beside + parity * (across - beside)
            target = across + parity * (beside - across)
            direct = [push(src, dst, me, source, send.at[1], recv), push(src, dst, me, target, send.at[2], recv)]
            relays = [
                [push(dst.at[source], dst, source, target, send.at[3], recv),
                 push(dst.at[source], dst, source, partner, forward.at[1], recv)],
                [push(dst.at[target], dst, target, partner, forward.at[2], recv)],
                [push(dst.at[far], dst, far, partner, forward.at[3], recv)],
            ]
        else:
            for t in range(1, n // 2):
                at = lax.rem(me - 2 * t + n, n)
                direct.append(push(src, dst, me, lax.rem(me + 2 * t, n), send.at[t], recv))
                relays.append([push(dst.at[at], dst, at, partner, forward.at[t], recv)])
        for t in range(n // 2):
            at = lax.rem(partner - 2 * t + n, n)
            arrivals.append(push(src, dst, at, partner, forward.at[t], recv))
        return direct + [own], relays, arrivals

    def relay(steps):
        for step in steps:
            step[0].wait_recv()
            for copy in step:
                copy.start()

    ik_direct, ik_relays, ik_arrivals = spread(ik_ref, ik_all, ik_s, ik_r, ik_f)
    lat_direct, lat_relays, lat_arrivals = spread(lat_ref, lat_all, lat_s, lat_r, lat_f)
    for copy in ik_direct + lat_direct:
        copy.start()
    ik_all[me] = ik_ref[...]
    lat_all[me] = lat_ref[...]
    w_t = jnp.transpose(w_ref[...])
    w_all[...] = w_t
    gains_all[...] = jnp.transpose(w_ref[pl.ds(pl.multiple_of(h * own_heads, own_heads), own_heads), :])
    relay(ik_relays)
    for copy in ik_arrivals:
        copy.wait_recv()
    for copy in loads:
        copy.wait()

    key_at = ks_ref[0] + lax.broadcasted_iota(jnp.int32, (part, keys), 1)
    row_at = qs_ref[0] + me * rows + lax.broadcasted_iota(jnp.int32, (part, keys), 0)

    def bias_of(chunk):
        return jnp.where(key_at <= row_at + chunk * part, 0.0, NEGATIVE)

    idx_keys = ik_all[...].reshape(keys, dim)
    w_rows = w_all[pl.ds(pl.multiple_of(h * part, part), part), :] * scale
    logits = jnp.zeros((part, keys), jnp.float32)
    group = 8
    for first in range(0, heads, group):
        stack = jnp.concatenate([iql[:, j * dim : (j + 1) * dim] for j in range(first, first + group)], axis=0)
        inner = lax.dot_general(stack, idx_keys, NT, preferred_element_type=jnp.float32)
        for j in range(group):
            gain = w_rows[:, first + j : first + j + 1]
            logits = logits + gain * jnp.maximum(inner[j * part : (j + 1) * part], 0.0)
        if first == 0:
            relay(lat_relays)
    logits = logits + bias_of(h)
    chance = jnp.exp(logits - jnp.max(logits, axis=-1, keepdims=True))
    chance = chance / jnp.sum(chance, axis=-1, keepdims=True)

    for copy in lat_arrivals:
        copy.wait_recv()
    for copy in q_loads:
        copy.wait()
    latents = lat_all[...].reshape(keys, width)
    blank = jnp.zeros((keys, shift), latents.dtype)
    k_even[...] = jnp.concatenate([latents, jnp.zeros((keys, key_width - width), latents.dtype)], axis=1)
    k_odd[...] = jnp.concatenate([jnp.zeros((keys, key_width - width), latents.dtype), latents], axis=1)

    step_pairs = math.gcd(pairs, 8)
    t_copies = []
    for k in range(1, hc + 1):
        chunk = others[k - 1] if k < hc else h
        bias = bias_of(chunk)

        def add_pairs(i, totals):
            q_rows = pl.ds(pl.multiple_of(chunk * part, part), part)
            q_pairs = pl.ds(i * step_pairs, step_pairs)
            for window, table in ((pl.ds(0, key_width), k_even), (pl.ds(shift, key_width), k_odd)):
                stack = q_buf[q_pairs, q_rows, window].reshape(step_pairs * part, key_width)
                scores = lax.dot_general(stack, table[...], NT, preferred_element_type=jnp.float32)
                scores = scores.reshape(step_pairs, part, keys) * (MAIN_SCALE * LOG2E) + bias[None]
                weights = jnp.exp2(scores - jnp.max(scores, axis=-1, keepdims=True))
                weights = weights * (1.0 / jnp.sum(weights, axis=-1, keepdims=True))
                totals = totals + jnp.sum(weights, axis=0)
            return totals

        totals = lax.fori_loop(0, pairs // step_pairs, add_pairs, jnp.zeros((part, keys), jnp.float32))
        if k < hc:
            t_send[k] = totals.astype(t_send.dtype)
            copy = pltpu.make_async_remote_copy(
                src_ref=t_send.at[k], dst_ref=t_recv.at[k], send_sem=t_s.at[k], recv_sem=t_r.at[k],
                device_id={"head": chunk}, device_id_type=MESH,
            )
            copy.start()
            t_copies.append(copy)
    for k in range(1, hc):
        t_copies[k - 1].wait_recv()
        totals = totals + t_recv[k].astype(jnp.float32)

    lane = lax.broadcasted_iota(jnp.int32, (part, rows), 1)
    line = lax.broadcasted_iota(jnp.int32, (part, rows), 0)
    cot = jnp.sum(jnp.where(lane == line + h * part, cot_ref[...], 0.0), axis=1, keepdims=True)
    upstream = (cot * (chance - totals * (1.0 / (2 * pairs * hc)))).astype(u_send.dtype)
    u_send[...] = upstream
    u_copies = []
    for k in range(1, hc):
        copy = pltpu.make_async_remote_copy(
            src_ref=u_send, dst_ref=u_all.at[h], send_sem=u_s.at[k], recv_sem=u_r.at[k],
            device_id={"head": others[k - 1]}, device_id_type=MESH,
        )
        copy.start()
        u_copies.append(copy)
    u_all[h] = upstream

    def stack_of(chunk):
        q_rows = pl.ds(pl.multiple_of(chunk * part, part), part)
        up = u_all[chunk].astype(jnp.float32)
        pieces = [iqg[q_rows, j * dim : (j + 1) * dim] for j in range(own_heads)]
        return q_rows, up, gains_all[q_rows, :], pieces, jnp.concatenate(pieces, axis=0)

    def add_key_grad(chunk, start):
        q_rows, up, gains, pieces, stack = stack_of(chunk)
        scaled = jnp.concatenate(
            [(pieces[j].astype(jnp.float32) * gains[:, j : j + 1]).astype(jnp.bfloat16) for j in range(own_heads)], axis=0
        )
        repeat = max(1, 128 // part)
        up_t = jnp.transpose(jnp.concatenate([up] * repeat, axis=0))
        up_wide = jnp.concatenate([up_t] * (own_heads // repeat), axis=1)
        inner_t = lax.dot_general(idx_keys, stack, NT, preferred_element_type=jnp.float32)
        grad_t = jnp.where(inner_t > 0.0, up_wide, 0.0).astype(jnp.bfloat16)
        term = jnp.dot(grad_t, scaled, preferred_element_type=jnp.float32)
        if start:
            dk[...] = term
        else:
            dk[...] += term

    column = lax.broadcasted_iota(jnp.int32, (part, gw_wide.shape[1]), 1)

    def put_query_grad(chunk):
        q_rows, up, gains, pieces, stack = stack_of(chunk)
        inner = lax.dot_general(stack, idx_keys, NT, preferred_element_type=jnp.float32)
        grad = jnp.where(inner.reshape(own_heads, part, keys) > 0.0, up[None], 0.0).astype(jnp.bfloat16)
        term = jnp.dot(grad.reshape(own_heads * part, keys), idx_keys, preferred_element_type=jnp.float32) * scale
        weight_grad = jnp.zeros((part, gw_wide.shape[1]), jnp.float32)
        for j in range(own_heads):
            own = term[j * part : (j + 1) * part]
            dot = jnp.sum(own * pieces[j].astype(jnp.float32), axis=1, keepdims=True)
            weight_grad = jnp.where(column == j, dot, weight_grad)
            gq_ref[q_rows, j * dim : (j + 1) * dim] = own * gains[:, j : j + 1]
        gw_wide[q_rows, :] = weight_grad

    add_key_grad(h, True)
    put_query_grad(h)
    for k in range(hc - 1, 0, -1):
        u_copies[k - 1].wait_recv()
        add_key_grad(sources[k - 1], False)
        if k == hc - 1:
            put_query_grad(sources[k - 1])
    dk_send[...] = (dk[...] * scale).astype(dk_send.dtype).reshape(n, block, dim)
    d_copies = []
    for t in range(1, n):
        peer = lax.rem(me + t, n)
        copy = pltpu.make_async_remote_copy(
            src_ref=dk_send.at[peer], dst_ref=dk_recv.at[t], send_sem=d_s.at[t], recv_sem=d_r.at[t],
            device_id={"ctx": peer}, device_id_type=MESH,
        )
        copy.start()
        d_copies.append(copy)
    for k in range(hc - 2, 0, -1):
        put_query_grad(sources[k - 1])
    gw_ref[...] = jnp.transpose(gw_wide[...])[:own_heads]

    own_block = dk[pl.ds(pl.multiple_of(me * block, block), block), :] * scale
    for t in range(1, n):
        d_copies[t - 1].wait_recv()
        own_block = own_block + dk_recv[t].astype(jnp.float32)
    z_send[...] = own_block.reshape(hc, block // hc, dim)
    z_copies = []
    for k in range(1, hc):
        peer = others[k - 1]
        copy = pltpu.make_async_remote_copy(
            src_ref=z_send.at[peer], dst_ref=z_recv.at[k], send_sem=z_s.at[k], recv_sem=z_r.at[k],
            device_id={"head": peer}, device_id_type=MESH,
        )
        copy.start()
        z_copies.append(copy)
    final = z_send[h]
    for k in range(1, hc):
        z_copies[k - 1].wait_recv()
        final = final + z_recv[k]
    gk_ref[...] = final

    relayed = [copy for step in ik_relays + lat_relays for copy in step]
    for copy in ik_direct + lat_direct + relayed + t_copies + u_copies + d_copies + z_copies:
        copy.wait_send()


def hand_out(gq_ref, gw_ref, gk_ref, gq_out, gw_out, gk_out):
    gq_out[...] = gq_ref[...]
    gw_out[...] = gw_ref[...]
    gk_out[...] = gk_ref[...]


def solution(mesh):
    n, hc = mesh.shape["ctx"], mesh.shape["head"]

    def step(main_query, latents, idx_query, idx_weight, idx_keys, kl_cotangent, query_start, key_start):
        rows, wide = main_query.shape
        block, width = latents.shape
        dim = idx_keys.shape[1]
        heads = idx_weight.shape[1]
        own_heads = heads // hc
        pairs = wide // (2 * width)
        keys = n * block
        key_width = pl.cdiv(width, 128) * 128
        part = rows // hc
        bf16, f32 = jnp.bfloat16, jnp.float32
        vmem = pl.BlockSpec(memory_space=pltpu.VMEM)
        smem = pl.BlockSpec(memory_space=pltpu.SMEM)
        hbm = pl.BlockSpec(memory_space=pl.ANY)
        dma = pltpu.SemaphoreType.DMA
        grads = pl.pallas_call(
            functools.partial(kernel, n, hc),
            out_shape=(
                jax.ShapeDtypeStruct((rows, heads * dim // hc), f32),
                jax.ShapeDtypeStruct((own_heads, rows), f32),
                jax.ShapeDtypeStruct((block // hc, dim), f32),
            ),
            in_specs=[smem, smem, hbm, vmem, hbm, vmem, vmem, vmem],
            out_specs=(vmem, vmem, vmem),
            scratch_shapes=[
                pltpu.VMEM((pairs, rows, 2 * width), bf16),
                pltpu.VMEM((part, heads * dim), bf16),
                pltpu.VMEM((rows, heads * dim // hc), bf16),
                pltpu.VMEM((n, block, width), bf16),
                pltpu.VMEM((n, block, dim), bf16),
                pltpu.VMEM((keys, key_width), bf16),
                pltpu.VMEM((keys, key_width), bf16),
                pltpu.VMEM((hc, part, keys), bf16),
                pltpu.VMEM((hc, part, keys), bf16),
                pltpu.VMEM((part, keys), bf16),
                pltpu.VMEM((hc, part, keys), bf16),
                pltpu.VMEM((rows, heads), f32),
                pltpu.VMEM((rows, heads // hc), f32),
                pltpu.VMEM((rows, 128), f32),
                pltpu.VMEM((keys, dim), f32),
                pltpu.VMEM((n, block, dim), bf16),
                pltpu.VMEM((n, block, dim), bf16),
                pltpu.VMEM((hc, block // hc, dim), f32),
                pltpu.VMEM((hc, block // hc, dim), f32),
                dma((pairs,)), dma((2,)),
                dma((n,)), dma((n,)), dma((n,)),
                dma((n,)), dma((n,)), dma((n,)),
                dma((hc,)), dma((hc,)), dma((hc,)), dma((hc,)),
                dma((n,)), dma((n,)), dma((hc,)), dma((hc,)),
            ],
            compiler_params=pltpu.CompilerParams(
                collective_id=0, has_side_effects=True, vmem_limit_bytes=60 * 2**20
            ),
        )(query_start, key_start, main_query, latents, idx_query, idx_weight.T, idx_keys, kl_cotangent.reshape(1, rows))
        strips = math.gcd(own_heads, 4)
        strip = own_heads // strips * dim
        by_strip = pl.BlockSpec((rows, strip), lambda i: (0, i))
        whole = [pl.BlockSpec(grad.shape, lambda i: (0, 0)) for grad in grads[1:]]
        grad_query, grad_weight, grad_keys = pl.pallas_call(
            hand_out,
            grid=(strips,),
            out_shape=tuple(jax.ShapeDtypeStruct(grad.shape, f32) for grad in grads),
            in_specs=[by_strip] + whole,
            out_specs=tuple([by_strip] + whole),
        )(*grads)
        return grad_query, grad_weight.T, grad_keys

    return jax.shard_map(
        step,
        mesh=mesh,
        in_specs=(
            P("ctx", "head"), P("ctx", None), P("ctx", None), P("ctx", None), P("ctx", None), P("ctx"), P(), P(),
        ),
        out_specs=(P("ctx", "head"), P("ctx", "head"), P(("ctx", "head"), None)),
        check_vma=False,
    )
```

```python
import functools
import math

import jax
import jax.numpy as jnp
from jax import lax
from jax.experimental import pallas as pl
from jax.experimental.pallas import tpu as pltpu
from jax.sharding import PartitionSpec as P

NEGATIVE = -1e30
LOG2E = math.log2(math.e)
MAIN_SCALE = 192.0 ** (-0.5)
MESH = pl.DeviceIdType.MESH
NT = (((1,), (1,)), ((), ()))


def kernel(
    n, hc, qs_ref, ks_ref, main_ref, lat_ref, iq_ref, w_ref, ik_ref, cot_ref,
    gq_ref, gw_ref, gk_ref,
    q_buf, iql, iqg, lat_all, ik_all, k_even, k_odd, t_send, t_recv, u_send, u_all, w_all, gains_all, gw_wide, dk, dk_send, dk_recv, z_send, z_recv,
    q_sem, i_sem, lat_s, lat_r, lat_f, ik_s, ik_r, ik_f, t_s, t_r, u_s, u_r, d_s, d_r, z_s, z_r,
):
    me = lax.axis_index("ctx")
    h = lax.axis_index("head")
    pairs, rows, pair_width = q_buf.shape
    width = pair_width // 2
    block, key_width = lat_ref.shape[0], k_even.shape[1]
    keys = n * block
    heads = w_ref.shape[0]
    dim = ik_ref.shape[1]
    part = rows // hc
    own_heads = heads // hc
    scale = dim ** (-0.5)
    shift = pair_width - key_width

    loads = [
        pltpu.make_async_copy(iq_ref.at[pl.ds(pl.multiple_of(h * part, part), part), :], iql, i_sem.at[0]),
        pltpu.make_async_copy(
            iq_ref.at[:, pl.ds(pl.multiple_of(h * own_heads * dim, own_heads * dim), own_heads * dim)], iqg, i_sem.at[1]
        ),
    ]
    q_loads = [
        pltpu.make_async_copy(main_ref.at[:, pl.ds(p * pair_width, pair_width)], q_buf.at[p], q_sem.at[p])
        for p in range(pairs)
    ]
    for copy in loads + q_loads:
        copy.start()

    barrier = pltpu.get_barrier_semaphore()
    for t in range(1, n):
        pl.semaphore_signal(barrier, inc=1, device_id={"ctx": lax.rem(me + t, n)}, device_id_type=MESH)
    for k in range(1, hc):
        pl.semaphore_signal(barrier, inc=1, device_id={"head": lax.rem(h + k, hc)}, device_id_type=MESH)
    pl.semaphore_wait(barrier, n - 1 + hc - 1)

    parity = lax.rem(me, 2)
    partner = me + 1 - 2 * parity
    if hc == 4:
        others = [hc - 1 - h, lax.rem(h + 2, hc), h + 1 - 2 * lax.rem(h, 2)]
        sources = others
    else:
        others = [lax.rem(h + k, hc) for k in range(1, hc)]
        sources = [lax.rem(h - k + hc, hc) for k in range(1, hc)]

    def push(src, dst, at, to, send, recv):
        return pltpu.make_async_remote_copy(
            src_ref=src, dst_ref=dst.at[at], send_sem=send, recv_sem=recv.at[at],
            device_id={"ctx": to}, device_id_type=MESH,
        )

    def spread(src, dst, send, recv, forward, hops):
        direct, relays, arrivals = [], [], []
        own = push(src, dst, me, partner, forward.at[0], recv)
        if hops and n == 8:
            beside = me + 2 - 4 * lax.rem(me // 2, 2)
            across = me + 4 - 8 * (me // 4)
            far = beside + across - me
            source = beside + parity * (across - beside)
            target = across + parity * (beside - across)
            direct = [push(src, dst, me, source, send.at[1], recv), push(src, dst, me, target, send.at[2], recv)]
            relays = [
                [push(dst.at[source], dst, source, target, send.at[3], recv),
                 push(dst.at[source], dst, source, partner, forward.at[1], recv)],
                [push(dst.at[target], dst, target, partner, forward.at[2], recv)],
                [push(dst.at[far], dst, far, partner, forward.at[3], recv)],
            ]
        else:
            for t in range(1, n // 2):
                at = lax.rem(me - 2 * t + n, n)
                direct.append(push(src, dst, me, lax.rem(me + 2 * t, n), send.at[t], recv))
                relays.append([push(dst.at[at], dst, at, partner, forward.at[t], recv)])
        for t in range(n // 2):
            at = lax.rem(partner - 2 * t + n, n)
            arrivals.append(push(src, dst, at, partner, forward.at[t], recv))
        return direct + [own], relays, arrivals

    def relay(steps):
        for step in steps:
            step[0].wait_recv()
            for copy in step:
                copy.start()

    ik_direct, ik_relays, ik_arrivals = spread(ik_ref, ik_all, ik_s, ik_r, ik_f, False)
    lat_direct, lat_relays, lat_arrivals = spread(lat_ref, lat_all, lat_s, lat_r, lat_f, True)
    for copy in ik_direct + lat_direct:
        copy.start()
    ik_all[me] = ik_ref[...]
    lat_all[me] = lat_ref[...]
    w_t = jnp.transpose(w_ref[...])
    w_all[...] = w_t
    gains_all[...] = jnp.transpose(w_ref[pl.ds(pl.multiple_of(h * own_heads, own_heads), own_heads), :])
    relay(ik_relays)
    relay(lat_relays[:-1])
    for copy in ik_arrivals:
        copy.wait_recv()
    for copy in loads:
        copy.wait()

    key_at = ks_ref[0] + lax.broadcasted_iota(jnp.int32, (part, keys), 1)
    row_at = qs_ref[0] + me * rows + lax.broadcasted_iota(jnp.int32, (part, keys), 0)

    def bias_of(chunk):
        return jnp.where(key_at <= row_at + chunk * part, 0.0, NEGATIVE)

    idx_keys = ik_all[...].reshape(keys, dim)
    w_rows = w_all[pl.ds(pl.multiple_of(h * part, part), part), :] * scale
    logits = jnp.zeros((part, keys), jnp.float32)
    group = 8
    for first in range(0, heads, group):
        stack = jnp.concatenate([iql[:, j * dim : (j + 1) * dim] for j in range(first, first + group)], axis=0)
        inner = lax.dot_general(stack, idx_keys, NT, preferred_element_type=jnp.float32)
        for j in range(group):
            gain = w_rows[:, first + j : first + j + 1]
            logits = logits + gain * jnp.maximum(inner[j * part : (j + 1) * part], 0.0)
    logits = logits + bias_of(h)
    chance = jnp.exp(logits - jnp.max(logits, axis=-1, keepdims=True))
    chance = chance / jnp.sum(chance, axis=-1, keepdims=True)

    relay(lat_relays[-1:])
    blank = jnp.zeros((block, key_width - width), lat_ref.dtype)

    def place(at):
        at_rows = pl.ds(pl.multiple_of(at * block, block), block)
        latent = lat_all[at]
        k_even[at_rows, :] = jnp.concatenate([latent, blank], axis=1)
        k_odd[at_rows, :] = jnp.concatenate([blank, latent], axis=1)

    for t in range(n // 2):
        place(lax.rem(me + 2 * t, n))
    for t in range(n // 2):
        lat_arrivals[t].wait_recv()
        place(lax.rem(partner - 2 * t + n, n))
    for copy in q_loads:
        copy.wait()

    step_pairs = math.gcd(pairs, 16)
    t_copies = []
    for k in range(1, hc + 1):
        chunk = others[k - 1] if k < hc else h
        bias = bias_of(chunk)

        def add_pairs(i, totals):
            q_rows = pl.ds(pl.multiple_of(chunk * part, part), part)
            q_pairs = pl.ds(i * step_pairs, step_pairs)
            for window, table in ((pl.ds(0, key_width), k_even), (pl.ds(shift, key_width), k_odd)):
                stack = q_buf[q_pairs, q_rows, window].reshape(step_pairs * part, key_width)
                scores = lax.dot_general(stack, table[...], NT, preferred_element_type=jnp.float32)
                scores = scores.reshape(step_pairs, part, keys) * (MAIN_SCALE * LOG2E) + bias[None]
                weights = jnp.exp2(scores - jnp.max(scores, axis=-1, keepdims=True))
                weights = weights * (1.0 / jnp.sum(weights, axis=-1, keepdims=True))
                totals = totals + jnp.sum(weights, axis=0)
            return totals

        totals = lax.fori_loop(0, pairs // step_pairs, add_pairs, jnp.zeros((part, keys), jnp.float32))
        if k < hc:
            t_send[k] = totals.astype(t_send.dtype)
            copy = pltpu.make_async_remote_copy(
                src_ref=t_send.at[k], dst_ref=t_recv.at[k], send_sem=t_s.at[k], recv_sem=t_r.at[k],
                device_id={"head": chunk}, device_id_type=MESH,
            )
            copy.start()
            t_copies.append(copy)
    for k in range(1, hc):
        t_copies[k - 1].wait_recv()
        totals = totals + t_recv[k].astype(jnp.float32)

    lane = lax.broadcasted_iota(jnp.int32, (part, rows), 1)
    line = lax.broadcasted_iota(jnp.int32, (part, rows), 0)
    cot = jnp.sum(jnp.where(lane == line + h * part, cot_ref[...], 0.0), axis=1, keepdims=True)
    upstream = (cot * (chance - totals * (1.0 / (2 * pairs * hc)))).astype(u_send.dtype)
    u_send[...] = upstream
    u_copies = []
    for k in range(1, hc):
        copy = pltpu.make_async_remote_copy(
            src_ref=u_send, dst_ref=u_all.at[h], send_sem=u_s.at[k], recv_sem=u_r.at[k],
            device_id={"head": others[k - 1]}, device_id_type=MESH,
        )
        copy.start()
        u_copies.append(copy)
    u_all[h] = upstream

    def stack_of(chunk):
        q_rows = pl.ds(pl.multiple_of(chunk * part, part), part)
        up = u_all[chunk].astype(jnp.float32)
        pieces = [iqg[q_rows, j * dim : (j + 1) * dim] for j in range(own_heads)]
        return q_rows, up, gains_all[q_rows, :], pieces, jnp.concatenate(pieces, axis=0)

    def add_key_grad(chunk, start):
        q_rows, up, gains, pieces, stack = stack_of(chunk)
        scaled = jnp.concatenate(
            [(pieces[j].astype(jnp.float32) * gains[:, j : j + 1]).astype(jnp.bfloat16) for j in range(own_heads)], axis=0
        )
        repeat = max(1, 128 // part)
        up_t = jnp.transpose(jnp.concatenate([up] * repeat, axis=0))
        up_wide = jnp.concatenate([up_t] * (own_heads // repeat), axis=1)
        inner_t = lax.dot_general(idx_keys, stack, NT, preferred_element_type=jnp.float32)
        grad_t = jnp.where(inner_t > 0.0, up_wide, 0.0).astype(jnp.bfloat16)
        term = jnp.dot(grad_t, scaled, preferred_element_type=jnp.float32)
        if start:
            dk[...] = term
        else:
            dk[...] += term

    column = lax.broadcasted_iota(jnp.int32, (part, gw_wide.shape[1]), 1)

    def put_query_grad(chunk):
        q_rows, up, gains, pieces, stack = stack_of(chunk)
        inner = lax.dot_general(stack, idx_keys, NT, preferred_element_type=jnp.float32)
        grad = jnp.where(inner.reshape(own_heads, part, keys) > 0.0, up[None], 0.0).astype(jnp.bfloat16)
        term = jnp.dot(grad.reshape(own_heads * part, keys), idx_keys, preferred_element_type=jnp.float32) * scale
        weight_grad = jnp.zeros((part, gw_wide.shape[1]), jnp.float32)
        for j in range(own_heads):
            own = term[j * part : (j + 1) * part]
            dot = jnp.sum(own * pieces[j].astype(jnp.float32), axis=1, keepdims=True)
            weight_grad = jnp.where(column == j, dot, weight_grad)
            gq_ref[q_rows, j * dim : (j + 1) * dim] = own * gains[:, j : j + 1]
        gw_wide[q_rows, :] = weight_grad

    add_key_grad(h, True)
    put_query_grad(h)
    for k in range(hc - 1, 0, -1):
        u_copies[k - 1].wait_recv()
        add_key_grad(sources[k - 1], False)
        if k == hc - 1:
            put_query_grad(sources[k - 1])
    dk_send[...] = (dk[...] * scale).astype(dk_send.dtype).reshape(n, block, dim)
    d_copies = []
    for t in range(1, n):
        peer = lax.rem(me + t, n)
        copy = pltpu.make_async_remote_copy(
            src_ref=dk_send.at[peer], dst_ref=dk_recv.at[t], send_sem=d_s.at[t], recv_sem=d_r.at[t],
            device_id={"ctx": peer}, device_id_type=MESH,
        )
        copy.start()
        d_copies.append(copy)
    for k in range(hc - 2, 0, -1):
        put_query_grad(sources[k - 1])
    gw_ref[...] = jnp.transpose(gw_wide[...])[:own_heads]

    own_block = dk[pl.ds(pl.multiple_of(me * block, block), block), :] * scale
    for t in range(1, n):
        d_copies[t - 1].wait_recv()
        own_block = own_block + dk_recv[t].astype(jnp.float32)
    z_send[...] = own_block.reshape(hc, block // hc, dim)
    z_copies = []
    for k in range(1, hc):
        peer = others[k - 1]
        copy = pltpu.make_async_remote_copy(
            src_ref=z_send.at[peer], dst_ref=z_recv.at[k], send_sem=z_s.at[k], recv_sem=z_r.at[k],
            device_id={"head": peer}, device_id_type=MESH,
        )
        copy.start()
        z_copies.append(copy)
    final = z_send[h]
    for k in range(1, hc):
        z_copies[k - 1].wait_recv()
        final = final + z_recv[k]
    gk_ref[...] = final

    relayed = [copy for step in ik_relays + lat_relays for copy in step]
    for copy in ik_direct + lat_direct + relayed + t_copies + u_copies + d_copies + z_copies:
        copy.wait_send()


def hand_out(gq_ref, gw_ref, gk_ref, gq_out, gw_out, gk_out):
    gq_out[...] = gq_ref[...]
    gw_out[...] = gw_ref[...]
    gk_out[...] = gk_ref[...]


def solution(mesh):
    n, hc = mesh.shape["ctx"], mesh.shape["head"]

    def step(main_query, latents, idx_query, idx_weight, idx_keys, kl_cotangent, query_start, key_start):
        rows, wide = main_query.shape
        block, width = latents.shape
        dim = idx_keys.shape[1]
        heads = idx_weight.shape[1]
        own_heads = heads // hc
        pairs = wide // (2 * width)
        keys = n * block
        key_width = pl.cdiv(width, 128) * 128
        part = rows // hc
        bf16, f32 = jnp.bfloat16, jnp.float32
        vmem = pl.BlockSpec(memory_space=pltpu.VMEM)
        smem = pl.BlockSpec(memory_space=pltpu.SMEM)
        hbm = pl.BlockSpec(memory_space=pl.ANY)
        dma = pltpu.SemaphoreType.DMA
        grads = pl.pallas_call(
            functools.partial(kernel, n, hc),
            out_shape=(
                jax.ShapeDtypeStruct((rows, heads * dim // hc), f32),
                jax.ShapeDtypeStruct((own_heads, rows), f32),
                jax.ShapeDtypeStruct((block // hc, dim), f32),
            ),
            in_specs=[smem, smem, hbm, vmem, hbm, vmem, vmem, vmem],
            out_specs=(vmem, vmem, vmem),
            scratch_shapes=[
                pltpu.VMEM((pairs, rows, 2 * width), bf16),
                pltpu.VMEM((part, heads * dim), bf16),
                pltpu.VMEM((rows, heads * dim // hc), bf16),
                pltpu.VMEM((n, block, width), bf16),
                pltpu.VMEM((n, block, dim), bf16),
                pltpu.VMEM((keys, key_width), bf16),
                pltpu.VMEM((keys, key_width), bf16),
                pltpu.VMEM((hc, part, keys), bf16),
                pltpu.VMEM((hc, part, keys), bf16),
                pltpu.VMEM((part, keys), bf16),
                pltpu.VMEM((hc, part, keys), bf16),
                pltpu.VMEM((rows, heads), f32),
                pltpu.VMEM((rows, heads // hc), f32),
                pltpu.VMEM((rows, 128), f32),
                pltpu.VMEM((keys, dim), f32),
                pltpu.VMEM((n, block, dim), bf16),
                pltpu.VMEM((n, block, dim), bf16),
                pltpu.VMEM((hc, block // hc, dim), f32),
                pltpu.VMEM((hc, block // hc, dim), f32),
                dma((pairs,)), dma((2,)),
                dma((n,)), dma((n,)), dma((n,)),
                dma((n,)), dma((n,)), dma((n,)),
                dma((hc,)), dma((hc,)), dma((hc,)), dma((hc,)),
                dma((n,)), dma((n,)), dma((hc,)), dma((hc,)),
            ],
            compiler_params=pltpu.CompilerParams(
                collective_id=0, has_side_effects=True, vmem_limit_bytes=60 * 2**20
            ),
        )(query_start, key_start, main_query, latents, idx_query, idx_weight.T, idx_keys, kl_cotangent.reshape(1, rows))
        strips = 1
        strip = own_heads // strips * dim
        by_strip = pl.BlockSpec((rows, strip), lambda i: (0, i))
        whole = [pl.BlockSpec(grad.shape, lambda i: (0, 0)) for grad in grads[1:]]
        grad_query, grad_weight, grad_keys = pl.pallas_call(
            hand_out,
            grid=(strips,),
            out_shape=tuple(jax.ShapeDtypeStruct(grad.shape, f32) for grad in grads),
            in_specs=[by_strip] + whole,
            out_specs=tuple([by_strip] + whole),
        )(*grads)
        return grad_query, grad_weight.T, grad_keys

    return jax.shard_map(
        step,
        mesh=mesh,
        in_specs=(
            P("ctx", "head"), P("ctx", None), P("ctx", None), P("ctx", None), P("ctx", None), P("ctx"), P(), P(),
        ),
        out_specs=(P("ctx", "head"), P("ctx", "head"), P(("ctx", "head"), None)),
        check_vma=False,
    )
```
